32 devices in a mesh: stream: 2 (over y), pages: 16 (over z, x, core).
Axes of the slice: x: 2, y: 2, z: 4, core: 2. Of those that a mesh axis runs over, the one named last changes fastest.
Arguments:
- features: bfloat16 [2, 16384, 768], P('stream', 'pages'), may hold values from -6 to 6
- box_bins: int32 [2, 3, 16384], P('stream', None, 'pages'), may hold values from 0 to 15
- text_mask: int32 [16384], P('pages'), may hold values from 0 to 1, as said below
- spatial_table: bfloat16 [256, 768], replicated, may hold values from -6 to 6
- joint_projection: bfloat16 [2, 768, 2304], P('stream', 'pages'), may hold values from -0.21875 to 0.21875
- spatial_projection: bfloat16 [2, 768, 1536], P('stream', 'pages'), may hold values from -0.21875 to 0.21875
- relative_table: float32 [2, 12, 93], P('stream'), may hold values from -3 to 3
- output_projection: bfloat16 [2, 768, 768], P('stream', 'pages'), may hold values from -1.75 to 1.75
- output_bias: float32 [2, 768], P('stream'), may hold values from -2 to 2
- norm_one_gain: float32 [2, 768], P('stream'), may hold values from 0.5 to 1.5
- norm_one_shift: float32 [2, 768], P('stream'), may hold values from -2 to 2
- up_weight: bfloat16 [2, 768, 3072], P('stream', 'pages'), may hold values from -0.21875 to 0.21875
- up_bias: float32 [2, 3072], P('stream'), may hold values from -3 to 3
- down_weight: bfloat16 [2, 3072, 768], P('stream', 'pages'), may hold values from -0.109375 to 0.109375
- down_bias: float32 [2, 768], P('stream'), may hold values from -2 to 2
- norm_two_gain: float32 [2, 768], P('stream'), may hold values from 0.5 to 1.5
- norm_two_shift: float32 [2, 768], P('stream'), may hold values from -2 to 2
- output_cotangent: bfloat16 [2, 16384, 768], P('stream', 'pages'), may hold values from -6 to 6
Outputs:
- layer_output: bfloat16 [2, 16384, 768], P('stream', 'pages')
- grad_features: float32 [2, 16384, 768], P('stream', 'pages')
- grad_joint: float32 [2, 768, 2304], P('stream', 'pages')
- grad_spatial: float32 [2, 768, 1536], P('stream', 'pages')
- grad_relative: float32 [2, 12, 93], P('stream')
- grad_output_projection: float32 [2, 768, 768], P('stream', 'pages')
- grad_output_bias: float32 [2, 768], P('stream')
- grad_norm_one_gain: float32 [2, 768], P('stream')
- grad_norm_one_shift: float32 [2, 768], P('stream')
- grad_up_weight: float32 [2, 768, 3072], P('stream', 'pages')
- grad_up_bias: float32 [2, 3072], P('stream')
- grad_down_weight: float32 [2, 3072, 768], P('stream', 'pages')
- grad_down_bias: float32 [2, 768], P('stream')
- grad_norm_two_gain: float32 [2, 768], P('stream')
- grad_norm_two_shift: float32 [2, 768], P('stream')
- grad_table: float32 [256, 768], replicated
The draws below stay inside these ranges and needn't reach their ends.
Inputs may be any that keep to these rules, and one draw needn't show every extreme that they name: `text_mask`: each page of 512 consecutive slots is 1 on its first 20 to 512 slots and 0 after; in every draw one page is all ones and one has exactly 20 ones.
All inputs are finite; a program needn't handle non-finite values.
Results may differ from the reference program's by a relative error of at most 0.018.
Values may be sent and summed in bfloat16 or wider, within the bound.
No kernel may reach another device: no remote copies, remote signals or barrier semaphores. Data moves between devices by JAX's collectives and lax.ppermute only.
A program may use at most 256 MiB of HBM per device.

```python
import jax
import jax.numpy as jnp
from jax import lax

D = 768
FF = 3072
HEADS = 12
HEAD_DIM = 64
SLOTS = 512
MIN_OCR = 20
BINS = 16
RELS = 93
NSP = 256
TOKENS = 16384


def draw_text_mask(key, part):
    page_count = TOKENS // SLOTS
    first_key, second_key = jax.random.split(key)
    lengths = jax.random.randint(first_key, (page_count,), MIN_OCR, SLOTS + 1)
    full_page = jax.random.randint(second_key, (), 0, page_count)
    page_ids = jnp.arange(page_count)
    lengths = jnp.where(page_ids == full_page, SLOTS, lengths)
    lengths = jnp.where(page_ids == (full_page + 1) % page_count, MIN_OCR, lengths)
    slot_ids = jnp.arange(SLOTS)
    return (slot_ids[None, :] < lengths[:, None]).astype(jnp.int32).reshape(TOKENS)


def with_ends(drawn, own_key, low, top_value):
    index_at = [jax.random.randint(jax.random.fold_in(own_key, axis), (), 0, length) for axis, length in enumerate(drawn.shape)]
    longest = drawn.shape.index(max(drawn.shape))
    next_to = index_at[:longest] + [(index_at[longest] + 1) % drawn.shape[longest]] + index_at[longest + 1:]
    return drawn.at[tuple(index_at)].set(low).at[tuple(next_to)].set(top_value)


def spiked(values, stream_key, source, target, shards_of, factor):
    owner, partner = [(jnp.arange(values.shape[axis_at]) // (values.shape[axis_at] // shards_of)).reshape([-1 if axis == axis_at else 1 for axis in range(values.ndim)]) for axis_at in (source, target)]
    chosen = jax.random.permutation(stream_key, shards_of)[partner]
    strong = (owner == chosen) | (owner == (partner + shards_of // 2) % shards_of)
    return jnp.where(strong, factor * values, values)


def levels(own_key, extent, cuts, smallest, top_value):
    def one(axis_at, parts):
        heights = jax.random.uniform(jax.random.fold_in(jax.random.fold_in(own_key, 6), axis_at), (parts,), jnp.float32, smallest / len(cuts), top_value / len(cuts))
        return jnp.repeat(jnp.exp(heights), extent[axis_at] // parts).reshape((-1,) + (1,) * (len(extent) - axis_at - 1))

    factor_of = one(*cuts[0])
    for cut in cuts[1:]:
        factor_of = factor_of * one(*cut)
    return factor_of


def gaussian(own_key, dims, width, reach, cuts=(), dtype=jnp.bfloat16):
    drawn = jax.random.normal(own_key, dims, jnp.float32) * width
    if len(cuts) > 0:
        drawn = levels(own_key, dims, cuts, -0.22, 0.18) * drawn
    return jnp.clip(drawn, min=-reach, max=reach).astype(dtype)


def bell_draw_with(stream_key, extent, scale, bound, cuts, heavy, dtype=jnp.bfloat16):
    values = scale * jax.random.normal(stream_key, extent, jnp.float32)
    if cuts:
        values = values * levels(stream_key, extent, cuts, -0.22, 0.18)
    return jnp.clip(spiked(values, jax.random.fold_in(stream_key, 3), *heavy), -bound, bound).astype(dtype)


def setup_inputs(seed: int = 0) -> dict:
    key_of = jax.random.split(jax.random.key(seed), 19)
    return {
        "features": bell_draw_with(key_of[0], (2, TOKENS, D), 1.0, 6.0, ((0, 2), (1, 16)), (1, 2, 16, 2.0)),
        "box_bins": with_ends(jax.random.randint(key_of[1], (2, 3, TOKENS), 0, BINS), jax.random.fold_in(key_of[1], 1), 0, BINS - 1).astype(jnp.int32),
        "text_mask": draw_text_mask(jax.random.fold_in(key_of[18], 71), 0),
        "spatial_table": gaussian(key_of[3], (NSP, D), 1.0, 6.0),
        "joint_projection": gaussian(key_of[4], (2, D, 3 * D), D ** -0.5, 0.21875, ((0, 2), (1, 16))),
        "spatial_projection": gaussian(key_of[5], (2, D, 2 * D), D ** -0.5, 0.21875, ((0, 2), (1, 16))),
        "relative_table": gaussian(key_of[6], (2, HEADS, RELS), 0.5, 3.0, ((0, 2),), jnp.float32),
        "output_projection": gaussian(key_of[7], (2, D, D), (D // 64) ** -0.5, 1.75, ((0, 2), (1, 16))),
        "output_bias": gaussian(key_of[8], (2, D), 0.3, 2.0, ((0, 2),), jnp.float32),
        "norm_one_gain": jnp.clip(1.0 + 0.1 * jax.random.normal(key_of[9], (2, D), jnp.float32), 0.5, 1.5),
        "norm_one_shift": gaussian(key_of[10], (2, D), 0.3, 2.0, ((0, 2),), jnp.float32),
        "up_weight": gaussian(key_of[11], (2, D, FF), D ** -0.5, 0.21875, ((0, 2), (1, 16))),
        "up_bias": gaussian(key_of[12], (2, FF), 0.5, 3.0, ((0, 2),), jnp.float32),
        "down_weight": gaussian(key_of[13], (2, FF, D), FF ** -0.5, 0.109375, ((0, 2), (1, 16))),
        "down_bias": gaussian(key_of[14], (2, D), 0.3, 2.0, ((0, 2),), jnp.float32),
        "norm_two_gain": jnp.clip(1.0 + 0.1 * jax.random.normal(key_of[15], (2, D), jnp.float32), 0.5, 1.5),
        "norm_two_shift": gaussian(key_of[16], (2, D), 0.3, 2.0, ((0, 2),), jnp.float32),
        "output_cotangent": gaussian(key_of[17], (2, TOKENS, D), 1.0, 6.0, ((0, 2), (1, 16))),
    }


@jax.custom_vjp
def low(v):
    return lax.optimization_barrier(v.astype(jnp.bfloat16)).astype(jnp.float32)

@jax.custom_vjp
def low_back(v):
    return v

def low_keep(v):
    return (low(v), None)

def low_pass(kept, grad):
    return (grad,)

def back_keep(v):
    return (v, None)

def back_low(kept, grad):
    return (low(grad),)
low.defvjp(low_keep, low_pass)
low_back.defvjp(back_keep, back_low)
highest = lax.Precision.HIGHEST
epsilon = 1e-05

def product(left_part, right_part):
    return jnp.dot(left_part, right_part, precision=highest, preferred_element_type=jnp.float32)

def layer_norm(values, gain, shift):
    centered = values - lax.optimization_barrier(jnp.mean(values, -1, keepdims=True))
    variance = lax.optimization_barrier(jnp.mean(centered * centered, -1, keepdims=True))
    return centered * lax.rsqrt(variance + epsilon) * gain + shift

def relative_bias(relative, page_bins):
    span_width = 2 * BINS - 1
    result = jnp.zeros((HEADS, SLOTS, SLOTS), jnp.float32)
    for family in range(3):
        position = page_bins[family][None, :] - page_bins[family][:, None] + (BINS - 1 + family * span_width)
        result = result + jnp.take(relative, position.astype(jnp.int32), axis=1)
    return result

def split_heads(array):
    return array.reshape(SLOTS, HEADS, HEAD_DIM)

def attend(feature, page_bins, key_valid, table_f, joint_weight, spatial_weight, relative, output_weight, output_shift):
    joint = low_back(low(product(feature, joint_weight)))
    cell_ids = page_bins[2] * BINS + page_bins[1]
    spatial = low_back(low(product(table_f[cell_ids], spatial_weight)))
    queries = jnp.concatenate([split_heads(joint[:, :D]), split_heads(spatial[:, :D])], -1)
    key_rows = jnp.concatenate([split_heads(joint[:, D:2 * D]), split_heads(spatial[:, D:])], -1)
    values = split_heads(joint[:, 2 * D:])
    dot_scores = jnp.einsum('ihe,jhe->hij', queries, key_rows, precision=highest)
    scores = low_back(dot_scores * HEAD_DIM ** (-0.5) + relative_bias(relative, page_bins))
    scores = jnp.where(key_valid[None, None, :] > 0, scores, -1000000000.0)
    shares = low(jax.nn.softmax(scores, axis=-1))
    mixture = jnp.einsum('hij,jhe->ihe', shares, values, precision=highest).reshape(SLOTS, D)
    mixture = low_back(low(mixture))
    return low_back(product(mixture, output_weight) + output_shift)

def page_layer(params, table_f, feature, page_bins, page_mask):
    joint_weight, spatial_weight, relative, output_weight, output_shift, gain_one, shift_one, upward, up_shift, downward, down_shift, gain_two, shift_two = params
    attended = []
    for stream_side in range(2):
        key_valid = page_mask if stream_side == 0 else jnp.ones_like(page_mask)
        attended.append(attend(feature[stream_side], page_bins[stream_side], key_valid, table_f, joint_weight[stream_side], spatial_weight[stream_side], relative[stream_side], output_weight[stream_side], output_shift[stream_side]))
    joined = attended[0] + attended[1]
    results = []
    for stream_side in range(2):
        hidden = layer_norm(feature[stream_side] + joined, gain_one[stream_side], shift_one[stream_side])
        pre_act = low_back(product(low(hidden), upward[stream_side]) + up_shift[stream_side])
        active = low(jax.nn.gelu(pre_act, approximate=False))
        branch = low_back(product(active, downward[stream_side]) + down_shift[stream_side])
        results.append(layer_norm(hidden + branch, gain_two[stream_side], shift_two[stream_side]))
    return jnp.stack(results)

def reference(features, box_bins, text_mask, spatial_table, joint_projection, spatial_projection, relative_table, output_projection, output_bias, norm_one_gain, norm_one_shift, up_weight, up_bias, down_weight, down_bias, norm_two_gain, norm_two_shift, output_cotangent):
    page_count = TOKENS // SLOTS
    float_type = jnp.float32
    params = tuple((item.astype(float_type) for item in (joint_projection, spatial_projection, relative_table, output_projection, output_bias, norm_one_gain, norm_one_shift, up_weight, up_bias, down_weight, down_bias, norm_two_gain, norm_two_shift)))
    table_f = spatial_table.astype(float_type)
    feats = features.astype(float_type).reshape(2, page_count, SLOTS, D).transpose(1, 0, 2, 3)
    cotangents = output_cotangent.astype(float_type).reshape(2, page_count, SLOTS, D).transpose(1, 0, 2, 3)
    bins_all = box_bins.reshape(2, 3, page_count, SLOTS).transpose(2, 0, 1, 3)
    masks = text_mask.reshape(page_count, SLOTS).astype(float_type)

    def page_step(running, page_data):
        feature, cotangent, page_bins, page_mask = page_data

        def forward(prm, tab, feat_in):
            return page_layer(prm, tab, feat_in, page_bins, page_mask)
        layer_out, pullback = jax.vjp(forward, params, table_f, feature)
        grad_params, grad_tab, grad_feat = pullback(cotangent)
        running = jax.tree.map(lambda first, second: first + second, running, (grad_params, grad_tab))
        return (running, (layer_out, grad_feat))
    initial = jax.tree.map(jnp.zeros_like, (params, table_f))
    (grad_params, grad_tab), (outputs, grad_feats) = lax.scan(page_step, initial, (feats, cotangents, bins_all, masks))
    layer_output = outputs.transpose(1, 0, 2, 3).reshape(2, TOKENS, D).astype(jnp.bfloat16)
    grad_features = grad_feats.transpose(1, 0, 2, 3).reshape(2, TOKENS, D)
    return (layer_output, grad_features, grad_params[0], grad_params[1], grad_params[2], grad_params[3], grad_params[4], grad_params[5], grad_params[6], grad_params[7], grad_params[8], grad_params[9], grad_params[10], grad_params[11], grad_params[12], grad_tab)
```

```python
import functools

import jax
import jax.numpy as jnp
from jax import lax
from jax.experimental import pallas as pl
from jax.experimental.pallas import tpu as pltpu
from jax.sharding import PartitionSpec as P

SLOTS = 512
BINS = 16
SPAN = 2 * BINS - 1
LEVELS = 3 * BINS
PAIR = 2
LANES = 128

highest = lax.Precision.HIGHEST
epsilon = 1e-05
masked_score = -1000000000.0
half = jnp.bfloat16
single = jnp.float32


def times(left, right):
    return jnp.dot(left, right, preferred_element_type=single)


def times_over_rows(left, right):
    return lax.dot_general(left, right, (((0,), (0,)), ((), ())), preferred_element_type=single)


def times_transposed(left, right):
    return lax.dot_general(left, right, (((1,), (1,)), ((), ())), preferred_element_type=single)


def layer_stats(values):
    centered = values - jnp.mean(values, -1, keepdims=True)
    inverse = lax.rsqrt(jnp.mean(centered * centered, -1, keepdims=True) + epsilon)
    return (centered * inverse, inverse)


def norm_back(grad_normed, normed, inverse):
    return inverse * (
        grad_normed
        - jnp.mean(grad_normed, -1, keepdims=True)
        - normed * jnp.mean(grad_normed * normed, -1, keepdims=True)
    )


def gelu_slope(values):
    cumulative = 0.5 * (1.0 + lax.erf(values * 0.7071067811865476))
    density = jnp.exp(-0.5 * values * values) * 0.3989422804014327
    return (values * cumulative, cumulative + values * density)


def flip(count, bit):
    return [(place, place ^ bit) for place in range(count)]


def swap_streams(array):
    return lax.ppermute(array, "stream", [(0, 1), (1, 0)])


def rounded(array, kept):
    return lax.reduce_precision(array, 8, 7) if kept == half else array


def bits_of(count):
    return [1 << step for step in range(count.bit_length() - 1)]


def sum_pages(array, count, kept):
    for bit in bits_of(count):
        array = rounded(array, kept)
        received = lax.ppermute(array.astype(kept), "pages", flip(count, bit))
        array = array + received.astype(array.dtype)
    return array


def grads_kernel(lhs_ref, rhs_ref, keep_ref, send_ref, tile_ref, sem, *, blocks, by_rows):
    place = lax.axis_index("pages")
    step = pl.program_id(0)
    rows, columns = tile_ref.shape[1] // blocks, tile_ref.shape[2]
    buffer = lax.rem(step, 2)
    lhs = lhs_ref[...]
    rhs = rhs_ref[...].reshape(rhs_ref.shape[-2:])

    def copies(at, action):
        for block in range(blocks):
            owner = at * blocks + block if by_rows else block
            column = 0 if by_rows else at * columns
            slot = place ^ owner
            index = ((slot >> 1) & 1) * 4 + (slot >> 2)
            source = tile_ref.at[lax.rem(at, 2), pl.ds(block * rows, rows)]

            def into(target):
                where = pl.ds(pl.multiple_of(column, LANES), columns)
                return pltpu.make_async_copy(
                    source, target.at[index, :, where], sem.at[lax.rem(at, 2), block]
                )

            @pl.when((slot & 1) == 0)
            def _():
                action(into(keep_ref))

            @pl.when((slot & 1) == 1)
            def _():
                action(into(send_ref))

    @pl.when(step >= 2)
    def _():
        copies(step - 2, lambda copy: copy.wait())

    tile_ref[buffer] = times_over_rows(lhs, rhs).astype(half)
    copies(step, lambda copy: copy.start())

    @pl.when(step == pl.num_programs(0) - 1)
    def _():
        @pl.when(step >= 1)
        def _():
            copies(step - 1, lambda copy: copy.wait())

        copies(step, lambda copy: copy.wait())


def weight_grads(lhs, rhs, count, tile, by_rows):
    rows_all = lhs.shape[1]
    columns = rhs.shape[1] if rhs.ndim == 2 else rhs.shape[0] * rhs.shape[2]
    rows = rows_all // count
    tokens = lhs.shape[0]
    if by_rows:
        steps, blocks, tile_shape = rows_all // tile, tile // rows, (tile, columns)
        lhs_spec = pl.BlockSpec((tokens, tile), lambda i: (0, i))
        rhs_spec = pl.BlockSpec((tokens, columns), lambda i: (0, 0))
    else:
        steps, blocks, tile_shape = columns // tile, count, (rows_all, tile)
        lhs_spec = pl.BlockSpec((tokens, rows_all), lambda i: (0, 0))
        rhs_spec = pl.BlockSpec((tokens, tile), lambda i: (0, i))
        if rhs.ndim == 3:
            rhs_spec = pl.BlockSpec((1, tokens, tile), lambda i: (i, 0, 0))
    out = jax.ShapeDtypeStruct((count // 2, rows, columns), half)
    return pl.pallas_call(
        functools.partial(grads_kernel, blocks=blocks, by_rows=by_rows),
        grid=(steps,),
        in_specs=[lhs_spec, rhs_spec],
        out_specs=[pl.BlockSpec(memory_space=pltpu.HBM)] * 2,
        out_shape=[out, out],
        scratch_shapes=[
            pltpu.VMEM((2, *tile_shape), half),
            pltpu.SemaphoreType.DMA((2, blocks)),
        ],
        compiler_params=pltpu.CompilerParams(vmem_limit_bytes=40 << 20),
        cost_estimate=pl.CostEstimate(
            flops=2 * tokens * rows_all * columns,
            bytes_accessed=2 * (tokens * (rows_all + columns) + rows_all * columns),
            transcendentals=0,
        ),
        name="weight_grads",
    )(lhs, rhs)


def scatter_sum(keep, send, count):
    received = lax.ppermute(send, "pages", flip(count, 1))
    quarter = keep.shape[0] // 2

    def added(part):
        return (keep[part].astype(single) + received[part].astype(single)).astype(half)

    send = added(slice(quarter, None))
    received_x = lax.ppermute(send, "pages", flip(count, 2))
    keep = added(slice(0, quarter))
    total = keep[0].astype(single) + received_x[0].astype(single)
    for slot in range(1, quarter):
        part = (keep[slot].astype(single) + received_x[slot].astype(single)).astype(half)
        total = total + lax.ppermute(part, "pages", flip(count, 4 * slot)).astype(single)
    return total


def summed_rows(lhs, rhs, count, tile, by_rows=False):
    if count == 16:
        return scatter_sum(*weight_grads(lhs, rhs, count, tile, by_rows), count)[None]
    if rhs.ndim == 3:
        rhs = jnp.concatenate(list(rhs), -1)
    local = times_over_rows(lhs, rhs).astype(half)
    return lax.psum_scatter(local[None], "pages", scatter_dimension=1, tiled=True).astype(single)


def wide_rows(first, second, extra, which, size):
    lanes = slice(which * size, (which + 1) * size)
    return jnp.concatenate([first[:, lanes], second[:, lanes], extra], axis=1)


def forward_kernel(
    q_ref, k_ref, v_ref, sq_ref, sk_ref, cells_ref, keyx_ref, rel_ref, out_w_ref, bias_ref,
    mix_ref, att_ref, send_ref, log_ref, *, scale, size
):
    pair = pl.program_id(0)
    cells = cells_ref[...]
    keyx = keyx_ref[...]
    q = (q_ref[...].astype(single) * scale).astype(half)
    sq = (times(cells, sq_ref[...]) * scale).astype(half)
    sk = times(cells, sk_ref[...]).astype(half)
    k = k_ref[...]
    values_t = jnp.transpose(v_ref[...])
    rel = times(keyx, rel_ref[...]).astype(half)
    mixed = []
    for which in range(PAIR):
        wide_q = wide_rows(q, sq, rel[:, which * LANES : (which + 1) * LANES], which, size)
        wide_k = wide_rows(k, sk, keyx, which, size)
        scores = times_transposed(wide_k, wide_q)
        largest = jnp.max(scores, 0, keepdims=True)
        lifted = jnp.exp(scores - largest)
        total = jnp.sum(lifted, 0, keepdims=True)
        log_ref[pl.ds(pair * PAIR + which, 1), :] = largest + jnp.log(total)
        part = times(values_t[which * size : (which + 1) * size], lifted.astype(half))
        mixed.append(part / total)
    mixture = jnp.transpose(jnp.concatenate(mixed, axis=0)).astype(half)
    mix_ref[...] = mixture

    @pl.when(pair == 0)
    def _():
        att_ref[...] = jnp.broadcast_to(bias_ref[...], att_ref.shape)

    att_ref[...] += times(mixture, out_w_ref[...])

    @pl.when(pair == pl.num_programs(0) - 1)
    def _():
        send_ref[...] = att_ref[...].astype(half)


def attend_page(page, joint_half, spatial_rows, cells, keyx, rel, out_w, bias, heads):
    width = out_w.shape[0]
    size = width // heads
    pairs = heads // PAIR
    block = PAIR * size
    table_rows = spatial_rows.shape[0]
    return pl.pallas_call(
        functools.partial(forward_kernel, scale=size**-0.5, size=size),
        grid=(pairs,),
        in_specs=[
            pl.BlockSpec((SLOTS, block), lambda h: (page, h)),
            pl.BlockSpec((SLOTS, block), lambda h: (page, pairs + h)),
            pl.BlockSpec((SLOTS, block), lambda h: (page, 2 * pairs + h)),
            pl.BlockSpec((table_rows, block), lambda h: (0, h)),
            pl.BlockSpec((table_rows, block), lambda h: (0, pairs + h)),
            pl.BlockSpec((SLOTS, table_rows), lambda h: (page, 0)),
            pl.BlockSpec((SLOTS, LANES), lambda h: (page, 0)),
            pl.BlockSpec((LANES, PAIR * LANES), lambda h: (0, h)),
            pl.BlockSpec((block, width), lambda h: (h, 0)),
            pl.BlockSpec((1, width), lambda h: (0, 0)),
        ],
        out_specs=[
            pl.BlockSpec((SLOTS, block), lambda h: (0, h)),
            pl.BlockSpec((SLOTS, width), lambda h: (0, 0)),
            pl.BlockSpec((SLOTS, width), lambda h: (0, 0)),
            pl.BlockSpec((heads, SLOTS), lambda h: (0, 0)),
        ],
        out_shape=[
            jax.ShapeDtypeStruct((SLOTS, width), half),
            jax.ShapeDtypeStruct((SLOTS, width), single),
            jax.ShapeDtypeStruct((SLOTS, width), half),
            jax.ShapeDtypeStruct((heads, SLOTS), single),
        ],
        compiler_params=pltpu.CompilerParams(vmem_limit_bytes=32 << 20),
        cost_estimate=pl.CostEstimate(
            flops=2 * heads * SLOTS * SLOTS * 6 * size,
            bytes_accessed=12 * SLOTS * width,
            transcendentals=heads * SLOTS * SLOTS,
        ),
        name="attend_page",
    )(
        joint_half, joint_half, joint_half, spatial_rows, spatial_rows, cells, keyx, rel, out_w,
        bias,
    )


def backward_kernel(
    q_ref, k_ref, v_ref, sq_ref, sk_ref, cells_ref, cells_t_ref, keyx_ref, rel_ref, log_ref,
    grad_ref, out_w_ref, *refs, scale, size, first
):
    if first:
        rows_ref, cell_q_ref, cell_k_ref, sums_ref = refs
    else:
        _, old_q_ref, old_k_ref, old_sums_ref, rows_ref, cell_q_ref, cell_k_ref, sums_ref = refs
    pair = pl.program_id(0)
    cells = cells_ref[...]
    cells_t = cells_t_ref[...]
    keyx = keyx_ref[...]
    q = (q_ref[...].astype(single) * scale).astype(half)
    sq = (times(cells, sq_ref[...]) * scale).astype(half)
    sk = times(cells, sk_ref[...]).astype(half)
    k = k_ref[...]
    v = v_ref[...]
    grad = times_transposed(grad_ref[...], out_w_ref[...]).astype(half)
    rel = times(keyx, rel_ref[...]).astype(half)
    gq, gsq, gk, gsk, gv = [], [], [], [], []
    for which in range(PAIR):
        lanes = slice(which * size, (which + 1) * size)
        wide_q = wide_rows(q, sq, rel[:, which * LANES : (which + 1) * LANES], which, size)
        wide_k = wide_rows(k, sk, keyx, which, size)
        scores = times_transposed(wide_k, wide_q)
        shares = jnp.exp(scores - log_ref[pl.ds(pair * PAIR + which, 1), :])
        grad_shares = times_transposed(v[:, lanes], grad[:, lanes])
        row_sums = jnp.sum(shares * grad_shares, 0, keepdims=True)
        grad_scores = (shares * (grad_shares - row_sums)).astype(half)
        gv.append(times(shares.astype(half), grad[:, lanes]))
        both = times(grad_scores, wide_q[:, : 2 * size])
        gk.append(both[:, :size])
        gsk.append(both[:, size:])
        wide_grad = times(jnp.transpose(wide_k), grad_scores)
        gq.append(wide_grad[:size] * scale)
        gsq.append(wide_grad[size : 2 * size] * scale)
        bins = wide_grad[2 * size : 2 * size + LEVELS]
        top = bins.astype(half)
        rest = (bins - top.astype(single)).astype(half)
        sums = times(top, keyx) + times(rest, keyx)
        part = slice(which * LEVELS, (which + 1) * LEVELS)
        sums_ref[0, part, :] = sums if first else sums + old_sums_ref[0, part, :]
    rows_ref[0] = jnp.transpose(jnp.concatenate(gq, axis=0)).astype(half)
    rows_ref[1] = jnp.concatenate(gk, axis=1).astype(half)
    rows_ref[2] = jnp.concatenate(gv, axis=1).astype(half)
    cell_q = times(cells_t, jnp.transpose(jnp.concatenate(gsq, axis=0)).astype(half))
    cell_k = times(cells_t, jnp.concatenate(gsk, axis=1).astype(half))
    cell_q_ref[...] = cell_q if first else cell_q + old_q_ref[...]
    cell_k_ref[...] = cell_k if first else cell_k + old_k_ref[...]


def attend_page_back(
    page, joint_half, spatial_rows, cells, cells_t, keyx, rel, log_total, grad, out_w, heads, before
):
    tokens = joint_half.shape[0]
    width = out_w.shape[0]
    size = width // heads
    pairs = heads // PAIR
    block = PAIR * size
    table_rows = spatial_rows.shape[0]
    cells_out = pl.BlockSpec((table_rows, block), lambda h: (0, h))
    sums_out = pl.BlockSpec((1, PAIR * LEVELS, LANES), lambda h: (h, 0, 0))
    first = before is None
    more = [] if first else [pl.BlockSpec(memory_space=pltpu.HBM), cells_out, cells_out, sums_out]
    return pl.pallas_call(
        functools.partial(backward_kernel, scale=size**-0.5, size=size, first=first),
        grid=(pairs,),
        in_specs=[
            pl.BlockSpec((SLOTS, block), lambda h: (page, h)),
            pl.BlockSpec((SLOTS, block), lambda h: (page, pairs + h)),
            pl.BlockSpec((SLOTS, block), lambda h: (page, 2 * pairs + h)),
            pl.BlockSpec((table_rows, block), lambda h: (0, h)),
            pl.BlockSpec((table_rows, block), lambda h: (0, pairs + h)),
            pl.BlockSpec((SLOTS, table_rows), lambda h: (page, 0)),
            pl.BlockSpec((table_rows, SLOTS), lambda h: (0, page)),
            pl.BlockSpec((SLOTS, LANES), lambda h: (page, 0)),
            pl.BlockSpec((LANES, PAIR * LANES), lambda h: (0, h)),
            pl.BlockSpec((heads, SLOTS), lambda h: (0, 0)),
            pl.BlockSpec((SLOTS, width), lambda h: (0, 0)),
            pl.BlockSpec((block, width), lambda h: (h, 0)),
            *more,
        ],
        out_specs=[
            pl.BlockSpec((3, SLOTS, block), lambda h: (0, page, h)), cells_out, cells_out, sums_out
        ],
        out_shape=[
            jax.ShapeDtypeStruct((3, tokens, width), half),
            jax.ShapeDtypeStruct((table_rows, width), single),
            jax.ShapeDtypeStruct((table_rows, width), single),
            jax.ShapeDtypeStruct((pairs, PAIR * LEVELS, LANES), single),
        ],
        input_output_aliases={} if first else {12: 0, 13: 1, 14: 2, 15: 3},
        compiler_params=pltpu.CompilerParams(vmem_limit_bytes=32 << 20),
        cost_estimate=pl.CostEstimate(
            flops=2 * heads * SLOTS * SLOTS * 16 * size,
            bytes_accessed=20 * SLOTS * width,
            transcendentals=heads * SLOTS * SLOTS,
        ),
        name="attend_page_back",
    )(
        joint_half, joint_half, joint_half, spatial_rows, spatial_rows, cells, cells_t, keyx, rel,
        log_total, grad, out_w, *(before or ()),
    )


def input_grad_kernel(rows_ref, weight_ref, resid_ref, out_ref):
    part = times_transposed(rows_ref[0], weight_ref[...])

    @pl.when(pl.program_id(0) == 0)
    def _():
        out_ref[...] = resid_ref[...] + part

    @pl.when(pl.program_id(0) > 0)
    def _():
        out_ref[...] += part


def input_grad(rows, weight, resid):
    parts, tokens, width = rows.shape
    return pl.pallas_call(
        input_grad_kernel,
        grid=(parts,),
        in_specs=[
            pl.BlockSpec((1, tokens, width), lambda n: (n, 0, 0)),
            pl.BlockSpec((width, width), lambda n: (0, n)),
            pl.BlockSpec((tokens, width), lambda n: (0, 0)),
        ],
        out_specs=pl.BlockSpec((tokens, width), lambda n: (0, 0)),
        out_shape=jax.ShapeDtypeStruct((tokens, width), single),
        compiler_params=pltpu.CompilerParams(vmem_limit_bytes=32 << 20),
        cost_estimate=pl.CostEstimate(
            flops=2 * parts * tokens * width * width,
            bytes_accessed=14 * tokens * width,
            transcendentals=0,
        ),
        name="input_grad",
    )(rows, weight, resid)


def level_offsets():
    row_bin = lax.broadcasted_iota(jnp.int32, (BINS, BINS, SPAN), 0)
    col_bin = lax.broadcasted_iota(jnp.int32, (BINS, BINS, SPAN), 1)
    offset = lax.broadcasted_iota(jnp.int32, (BINS, BINS, SPAN), 2)
    return (col_bin - row_bin + BINS - 1 == offset).astype(single)


def relative_columns(relative, offsets):
    heads = relative.shape[0]
    tables = relative.reshape(heads, 3, SPAN)
    squares = jnp.einsum("hfr,acr->fahc", tables, offsets, precision=highest)
    blocks = jnp.zeros((3, BINS, heads, 3, BINS), single)
    for family in range(3):
        blocks = blocks.at[family, :, :, family].set(squares[family])
    blocks = blocks.reshape(LEVELS, heads, LEVELS)
    top = blocks.astype(half)
    low = (blocks - top.astype(single)).astype(half)
    ones = (lax.broadcasted_iota(jnp.int32, (LEVELS, heads, 1), 0) < BINS).astype(half)
    spare = jnp.zeros((LEVELS, heads, LANES - 2 * LEVELS - 1), half)
    columns = jnp.concatenate([top, low, ones, spare], -1).reshape(LEVELS, heads * LANES)
    return jnp.pad(columns, ((0, LANES - LEVELS), (0, 0)))


def key_columns(bins, key_valid):
    tokens = bins.shape[1]
    level = lax.broadcasted_iota(jnp.int32, (tokens, BINS), 1)
    onehot = jnp.concatenate([(bins[f][:, None] == level).astype(half) for f in range(3)], -1)
    masked = jnp.where(key_valid > 0, 0.0, masked_score).astype(half)[:, None]
    spare = jnp.zeros((tokens, LANES - 2 * LEVELS - 1), half)
    return jnp.concatenate([onehot, onehot, masked, spare], -1)


def relative_grad(sums, offsets):
    pairs = sums.shape[0]
    sums = sums.reshape(pairs * PAIR, LEVELS, LANES)[:, :, :LEVELS]
    pieces = []
    for family in range(3):
        part = slice(family * BINS, (family + 1) * BINS)
        pieces.append(jnp.einsum("hca,acr->hr", sums[:, part, part], offsets, precision=highest))
    return jnp.concatenate(pieces, -1)


def body(
    features,
    box_bins,
    text_mask,
    spatial_table,
    joint_projection,
    spatial_projection,
    relative_table,
    output_projection,
    output_bias,
    norm_one_gain,
    norm_one_shift,
    up_weight,
    up_bias,
    down_weight,
    down_bias,
    norm_two_gain,
    norm_two_shift,
    output_cotangent,
    *,
    count,
):
    tokens, width = features.shape[1:]
    heads = relative_table.shape[1]
    table_rows = spatial_table.shape[0]
    page_count = tokens // SLOTS
    stream_side = lax.axis_index("stream")
    key_valid = jnp.where(stream_side == 0, text_mask, jnp.ones_like(text_mask))
    inputs = features[0]
    bins = box_bins[0]
    gain_one, shift_one = norm_one_gain[0], norm_one_shift[0]
    gain_two, shift_two = norm_two_gain[0], norm_two_shift[0]

    early = jnp.concatenate([joint_projection, spatial_projection, output_projection], -1)
    early = lax.all_gather(early, "pages", axis=1, tiled=True)[0]
    full_joint = early[:, : 3 * width]
    full_spatial = early[:, 3 * width : 5 * width]
    full_output = early[:, 5 * width :]
    full_up = lax.all_gather(up_weight, "pages", axis=1, tiled=True)[0]
    full_down = lax.all_gather(down_weight, "pages", axis=1, tiled=True)[0]

    offsets = level_offsets()
    rel = relative_columns(relative_table[0], offsets)
    keyx = key_columns(bins, key_valid)
    cell_ids = bins[2] * BINS + bins[1]
    cells = (cell_ids[:, None] == lax.broadcasted_iota(jnp.int32, (tokens, table_rows), 1)).astype(half)
    cells_t = (cell_ids[None, :] == lax.broadcasted_iota(jnp.int32, (table_rows, tokens), 0)).astype(half)

    joint_half = times(inputs, full_joint).astype(half)
    spatial_rows = times(spatial_table, full_spatial).astype(half)
    mixtures, logs, joined = [], [], []
    for page in range(page_count):
        mixture, own, sent, log_total = attend_page(
            page, joint_half, spatial_rows, cells, keyx, rel, full_output, output_bias, heads
        )
        mixtures.append(mixture)
        logs.append(log_total)
        joined.append(own + swap_streams(sent).astype(single))
    mixture = jnp.concatenate(mixtures, 0)
    joined = jnp.concatenate(joined, 0)

    normed_one, inverse_one = layer_stats(inputs.astype(single) + joined)
    hidden = normed_one * gain_one + shift_one
    hidden_half = hidden.astype(half)
    activated, slope = gelu_slope(times(hidden_half, full_up) + up_bias[0])
    active_half = activated.astype(half)
    normed_two, inverse_two = layer_stats(hidden + (times(active_half, full_down) + down_bias[0]))
    layer_output = (normed_two * gain_two + shift_two).astype(half)
    upstream = output_cotangent[0].astype(single)
    grad_resid_two = norm_back(upstream * gain_two, normed_two, inverse_two)
    grad_branch = grad_resid_two.astype(half)
    grad_down = summed_rows(active_half, grad_branch, count, width, by_rows=True)
    grad_pre = (times_transposed(grad_branch, full_down) * slope).astype(half)
    grad_hidden = grad_resid_two + times_transposed(grad_pre, full_up)
    grad_resid_one = norm_back(grad_hidden * gain_one, normed_one, inverse_one)
    grad_up = summed_rows(hidden_half, grad_pre, count, width)

    grad_attention, before = [], None
    for page in range(page_count):
        part = grad_resid_one[page * SLOTS : (page + 1) * SLOTS]
        part = (part + swap_streams(part.astype(half)).astype(single)).astype(half)
        grad_attention.append(part)
        before = attend_page_back(
            page, joint_half, spatial_rows, cells, cells_t, keyx, rel, logs[page], part, full_output,
            heads, before,
        )
    grad_rows, cell_q, cell_k, bin_sums = before
    grad_attention = jnp.concatenate(grad_attention, 0)
    grad_output = summed_rows(mixture, grad_attention, count, width)
    grad_joint = summed_rows(inputs, grad_rows, count, width)
    cell_half = jnp.concatenate([cell_q, cell_k], 1).astype(half)
    grad_spatial = summed_rows(spatial_table, cell_half, count, width)
    grad_table = sum_pages(times_transposed(cell_half, full_spatial), count, half)
    grad_table = rounded(grad_table, half)
    grad_table = grad_table + swap_streams(grad_table.astype(half)).astype(single)
    grad_features = input_grad(grad_rows, full_joint, grad_resid_one)

    small = [
        jnp.sum(grad_hidden * normed_one, 0),
        jnp.sum(grad_hidden, 0),
        jnp.sum(grad_attention.astype(single), 0),
        jnp.sum(grad_pre.astype(single), 0),
        jnp.sum(grad_branch.astype(single), 0),
        jnp.sum(upstream * normed_two, 0),
        jnp.sum(upstream, 0),
        relative_grad(bin_sums, offsets).reshape(-1),
    ]
    ends = []
    for piece in small:
        ends.append((ends[-1] if ends else 0) + piece.shape[0])
    packed = jnp.concatenate(small)
    packed = jnp.pad(packed, (0, -ends[-1] % (8 * LANES))).reshape(-1, LANES)
    packed = sum_pages(packed, count, single).reshape(-1)
    small = [packed[end - piece.shape[0] : end] for end, piece in zip(ends, small)]

    return (
        layer_output[None],
        grad_features[None],
        grad_joint,
        grad_spatial,
        small[7].reshape(relative_table.shape),
        grad_output,
        small[2][None],
        small[0][None],
        small[1][None],
        grad_up,
        small[3][None],
        grad_down,
        small[4][None],
        small[5][None],
        small[6][None],
        grad_table,
    )


def solution(mesh):
    rows = P("stream", "pages", None)
    vector = P("stream", None)
    placed = (
        rows,
        P("stream", None, "pages"),
        P("pages"),
        P(),
        rows,
        rows,
        P("stream", None, None),
        rows,
        vector,
        vector,
        vector,
        rows,
        vector,
        rows,
        vector,
        vector,
        vector,
        rows,
    )
    out_specs = (
        rows,
        rows,
        rows,
        rows,
        P("stream", None, None),
        rows,
        vector,
        vector,
        vector,
        rows,
        vector,
        rows,
        vector,
        vector,
        vector,
        P(),
    )
    return jax.shard_map(
        functools.partial(body, count=mesh.shape["pages"]),
        mesh=mesh,
        in_specs=placed,
        out_specs=out_specs,
        check_vma=False,
    )
```

```python
import functools

import jax
import jax.numpy as jnp
from jax import lax
from jax.experimental import pallas as pl
from jax.experimental.pallas import tpu as pltpu
from jax.sharding import PartitionSpec as P

SLOTS = 512
BINS = 16
SPAN = 2 * BINS - 1
LEVELS = 3 * BINS
PAIR = 2
LANES = 128

highest = lax.Precision.HIGHEST
epsilon = 1e-05
masked_score = -1000000000.0
half = jnp.bfloat16
single = jnp.float32


def times(left, right):
    return jnp.dot(left, right, preferred_element_type=single)


def times_over_rows(left, right):
    return lax.dot_general(left, right, (((0,), (0,)), ((), ())), preferred_element_type=single)


def times_transposed(left, right):
    return lax.dot_general(left, right, (((1,), (1,)), ((), ())), preferred_element_type=single)


def layer_stats(values):
    centered = values - jnp.mean(values, -1, keepdims=True)
    inverse = lax.rsqrt(jnp.mean(centered * centered, -1, keepdims=True) + epsilon)
    return (centered * inverse, inverse)


def norm_back(grad_normed, normed, inverse):
    return inverse * (
        grad_normed
        - jnp.mean(grad_normed, -1, keepdims=True)
        - normed * jnp.mean(grad_normed * normed, -1, keepdims=True)
    )


def gelu_slope(values):
    cumulative = 0.5 * (1.0 + lax.erf(values * 0.7071067811865476))
    density = jnp.exp(-0.5 * values * values) * 0.3989422804014327
    return (values * cumulative, cumulative + values * density)


def flip(count, bit):
    return [(place, place ^ bit) for place in range(count)]


def swap_streams(array):
    return lax.ppermute(array, "stream", [(0, 1), (1, 0)])


def rounded(array, kept):
    return lax.reduce_precision(array, 8, 7) if kept == half else array


def bits_of(count):
    return [1 << step for step in range(count.bit_length() - 1)]


def sum_pages(array, count, kept):
    for bit in bits_of(count):
        array = rounded(array, kept)
        received = lax.ppermute(array.astype(kept), "pages", flip(count, bit))
        array = array + received.astype(array.dtype)
    return array


def grads_kernel(lhs_ref, rhs_ref, keep_ref, send_ref, tile_ref, sem, *, blocks, by_rows):
    place = lax.axis_index("pages")
    step = pl.program_id(0)
    rows, columns = tile_ref.shape[1] // blocks, tile_ref.shape[2]
    buffer = lax.rem(step, 2)
    lhs = lhs_ref[...]
    rhs = rhs_ref[...].reshape(rhs_ref.shape[-2:])

    def copies(at, action):
        for block in range(blocks):
            owner = at * blocks + block if by_rows else block
            column = 0 if by_rows else at * columns
            slot = place ^ owner
            index = ((slot >> 1) & 1) * 4 + (slot >> 2)
            source = tile_ref.at[lax.rem(at, 2), pl.ds(block * rows, rows)]

            def into(target):
                where = pl.ds(pl.multiple_of(column, LANES), columns)
                return pltpu.make_async_copy(
                    source, target.at[index, :, where], sem.at[lax.rem(at, 2), block]
                )

            @pl.when((slot & 1) == 0)
            def _():
                action(into(keep_ref))

            @pl.when((slot & 1) == 1)
            def _():
                action(into(send_ref))

    @pl.when(step >= 2)
    def _():
        copies(step - 2, lambda copy: copy.wait())

    tile_ref[buffer] = times_over_rows(lhs, rhs).astype(half)
    copies(step, lambda copy: copy.start())

    @pl.when(step == pl.num_programs(0) - 1)
    def _():
        @pl.when(step >= 1)
        def _():
            copies(step - 1, lambda copy: copy.wait())

        copies(step, lambda copy: copy.wait())


def weight_grads(lhs, rhs, count, tile, by_rows):
    rows_all = lhs.shape[1]
    columns = rhs.shape[1] if rhs.ndim == 2 else rhs.shape[0] * rhs.shape[2]
    rows = rows_all // count
    tokens = lhs.shape[0]
    if by_rows:
        steps, blocks, tile_shape = rows_all // tile, tile // rows, (tile, columns)
        lhs_spec = pl.BlockSpec((tokens, tile), lambda i: (0, i))
        rhs_spec = pl.BlockSpec((tokens, columns), lambda i: (0, 0))
    else:
        steps, blocks, tile_shape = columns // tile, count, (rows_all, tile)
        lhs_spec = pl.BlockSpec((tokens, rows_all), lambda i: (0, 0))
        rhs_spec = pl.BlockSpec((tokens, tile), lambda i: (0, i))
        if rhs.ndim == 3:
            rhs_spec = pl.BlockSpec((1, tokens, tile), lambda i: (i, 0, 0))
    out = jax.ShapeDtypeStruct((count // 2, rows, columns), half)
    return pl.pallas_call(
        functools.partial(grads_kernel, blocks=blocks, by_rows=by_rows),
        grid=(steps,),
        in_specs=[lhs_spec, rhs_spec],
        out_specs=[pl.BlockSpec(memory_space=pltpu.HBM)] * 2,
        out_shape=[out, out],
        scratch_shapes=[
            pltpu.VMEM((2, *tile_shape), half),
            pltpu.SemaphoreType.DMA((2, blocks)),
        ],
        compiler_params=pltpu.CompilerParams(vmem_limit_bytes=40 << 20),
        cost_estimate=pl.CostEstimate(
            flops=2 * tokens * rows_all * columns,
            bytes_accessed=2 * (tokens * (rows_all + columns) + rows_all * columns),
            transcendentals=0,
        ),
        name="weight_grads",
    )(lhs, rhs)


class RowSum:
    def __init__(self, lhs, rhs, count, tile, by_rows=False):
        self.count = count
        self.split = count == 16
        if self.split:
            self.keep, self.send = weight_grads(lhs, rhs, count, tile, by_rows)
            self.held = [self.send]
        else:
            if rhs.ndim == 3:
                rhs = jnp.concatenate(list(rhs), -1)
            local = times_over_rows(lhs, rhs).astype(half)
            local = lax.psum_scatter(local[None], "pages", scatter_dimension=1, tiled=True)
            self.held = [local.astype(single)]

    def cores(self):
        if self.split:
            self.held = [lax.ppermute(self.held[0], "pages", flip(self.count, 1))]

    def across_x(self):
        if self.split:
            quarter = self.keep.shape[0] // 2
            received = self.held[0]
            added = [
                (self.keep[part].astype(single) + received[part].astype(single)).astype(half)
                for part in (slice(0, quarter), slice(quarter, None))
            ]
            self.keep = added[0]
            self.held = [lax.ppermute(added[1], "pages", flip(self.count, 2))]

    def across_z(self):
        if self.split:
            received = self.held[0]
            self.total = self.keep[0].astype(single) + received[0].astype(single)
            self.held = []
            for slot in range(1, self.keep.shape[0]):
                part = self.keep[slot].astype(single) + received[slot].astype(single)
                self.held.append(
                    lax.ppermute(part.astype(half), "pages", flip(self.count, 4 * slot))
                )

    def result(self):
        if not self.split:
            return self.held[0]
        total = self.total
        for part in self.held:
            total = total + part.astype(single)
        return total[None]


def after(array, *sums):
    held = [part for one in sums for part in one.held]
    array, *held = lax.optimization_barrier((array, *held))
    for one in sums:
        one.held, held = held[: len(one.held)], held[len(one.held) :]
    return array


def sum_table(array, count):
    rows = array.shape[0] // 2
    core = lax.rem(lax.axis_index("pages"), 2)
    mine = lax.dynamic_slice_in_dim(array, core * rows, rows, 0)
    other = lax.dynamic_slice_in_dim(array, (1 - core) * rows, rows, 0)
    mine = mine + lax.ppermute(other.astype(half), "pages", flip(count, 1)).astype(single)
    for bit in bits_of(count)[1:]:
        mine = rounded(mine, half)
        mine = mine + lax.ppermute(mine.astype(half), "pages", flip(count, bit)).astype(single)
    mine = rounded(mine, half)
    mine = rounded(mine + swap_streams(mine.astype(half)).astype(single), half)
    other = lax.ppermute(mine.astype(half), "pages", flip(count, 1)).astype(single)
    return jnp.where(core == 0, jnp.concatenate([mine, other]), jnp.concatenate([other, mine]))


def wide_rows(first, second, extra, which, size):
    lanes = slice(which * size, (which + 1) * size)
    return jnp.concatenate([first[:, lanes], second[:, lanes], extra], axis=1)


def forward_kernel(
    q_ref, k_ref, v_ref, sq_ref, sk_ref, cells_ref, keyx_ref, rel_ref, out_w_ref, bias_ref,
    mix_ref, att_ref, send_ref, log_ref, *, scale, size
):
    pair = pl.program_id(0)
    cells = cells_ref[...]
    keyx = keyx_ref[...]
    q = (q_ref[...].astype(single) * scale).astype(half)
    sq = (times(cells, sq_ref[...]) * scale).astype(half)
    sk = times(cells, sk_ref[...]).astype(half)
    k = k_ref[...]
    values_t = jnp.transpose(v_ref[...])
    rel = times(keyx, rel_ref[...]).astype(half)
    mixed = []
    for which in range(PAIR):
        wide_q = wide_rows(q, sq, rel[:, which * LANES : (which + 1) * LANES], which, size)
        wide_k = wide_rows(k, sk, keyx, which, size)
        scores = times_transposed(wide_k, wide_q)
        largest = jnp.max(scores, 0, keepdims=True)
        lifted = jnp.exp(scores - largest)
        total = jnp.sum(lifted, 0, keepdims=True)
        log_ref[pl.ds(pair * PAIR + which, 1), :] = largest + jnp.log(total)
        part = times(values_t[which * size : (which + 1) * size], lifted.astype(half))
        mixed.append(part / total)
    mixture = jnp.transpose(jnp.concatenate(mixed, axis=0)).astype(half)
    mix_ref[...] = mixture

    @pl.when(pair == 0)
    def _():
        att_ref[...] = jnp.broadcast_to(bias_ref[...], att_ref.shape)

    att_ref[...] += times(mixture, out_w_ref[...])

    @pl.when(pair == pl.num_programs(0) - 1)
    def _():
        send_ref[...] = att_ref[...].astype(half)


def attend_page(page, joint_half, spatial_rows, cells, keyx, rel, out_w, bias, heads):
    width = out_w.shape[0]
    size = width // heads
    pairs = heads // PAIR
    block = PAIR * size
    table_rows = spatial_rows.shape[0]
    return pl.pallas_call(
        functools.partial(forward_kernel, scale=size**-0.5, size=size),
        grid=(pairs,),
        in_specs=[
            pl.BlockSpec((SLOTS, block), lambda h: (page, h)),
            pl.BlockSpec((SLOTS, block), lambda h: (page, pairs + h)),
            pl.BlockSpec((SLOTS, block), lambda h: (page, 2 * pairs + h)),
            pl.BlockSpec((table_rows, block), lambda h: (0, h)),
            pl.BlockSpec((table_rows, block), lambda h: (0, pairs + h)),
            pl.BlockSpec((SLOTS, table_rows), lambda h: (page, 0)),
            pl.BlockSpec((SLOTS, LANES), lambda h: (page, 0)),
            pl.BlockSpec((LANES, PAIR * LANES), lambda h: (0, h)),
            pl.BlockSpec((block, width), lambda h: (h, 0)),
            pl.BlockSpec((1, width), lambda h: (0, 0)),
        ],
        out_specs=[
            pl.BlockSpec((SLOTS, block), lambda h: (0, h)),
            pl.BlockSpec((SLOTS, width), lambda h: (0, 0)),
            pl.BlockSpec((SLOTS, width), lambda h: (0, 0)),
            pl.BlockSpec((heads, SLOTS), lambda h: (0, 0)),
        ],
        out_shape=[
            jax.ShapeDtypeStruct((SLOTS, width), half),
            jax.ShapeDtypeStruct((SLOTS, width), single),
            jax.ShapeDtypeStruct((SLOTS, width), half),
            jax.ShapeDtypeStruct((heads, SLOTS), single),
        ],
        compiler_params=pltpu.CompilerParams(vmem_limit_bytes=32 << 20),
        cost_estimate=pl.CostEstimate(
            flops=2 * heads * SLOTS * SLOTS * 6 * size,
            bytes_accessed=12 * SLOTS * width,
            transcendentals=heads * SLOTS * SLOTS,
        ),
        name="attend_page",
    )(
        joint_half, joint_half, joint_half, spatial_rows, spatial_rows, cells, keyx, rel, out_w,
        bias,
    )


def backward_kernel(
    q_ref, k_ref, v_ref, sq_ref, sk_ref, cells_ref, cells_t_ref, keyx_ref, rel_ref, log_ref,
    grad_ref, out_w_ref, *refs, scale, size, first
):
    if first:
        rows_ref, cell_q_ref, cell_k_ref, sums_ref = refs
    else:
        _, old_q_ref, old_k_ref, old_sums_ref, rows_ref, cell_q_ref, cell_k_ref, sums_ref = refs
    pair = pl.program_id(0)
    cells = cells_ref[...]
    cells_t = cells_t_ref[...]
    keyx = keyx_ref[...]
    q = (q_ref[...].astype(single) * scale).astype(half)
    sq = (times(cells, sq_ref[...]) * scale).astype(half)
    sk = times(cells, sk_ref[...]).astype(half)
    k = k_ref[...]
    v = v_ref[...]
    grad = times_transposed(grad_ref[...], out_w_ref[...]).astype(half)
    rel = times(keyx, rel_ref[...]).astype(half)
    gq, gsq, gk, gsk, gv = [], [], [], [], []
    for which in range(PAIR):
        lanes = slice(which * size, (which + 1) * size)
        wide_q = wide_rows(q, sq, rel[:, which * LANES : (which + 1) * LANES], which, size)
        wide_k = wide_rows(k, sk, keyx, which, size)
        scores = times_transposed(wide_k, wide_q)
        shares = jnp.exp(scores - log_ref[pl.ds(pair * PAIR + which, 1), :])
        grad_shares = times_transposed(v[:, lanes], grad[:, lanes])
        row_sums = jnp.sum(shares * grad_shares, 0, keepdims=True)
        grad_scores = (shares * (grad_shares - row_sums)).astype(half)
        gv.append(times(shares.astype(half), grad[:, lanes]))
        both = times(grad_scores, wide_q[:, : 2 * size])
        gk.append(both[:, :size])
        gsk.append(both[:, size:])
        wide_grad = times(jnp.transpose(wide_k), grad_scores)
        gq.append(wide_grad[:size] * scale)
        gsq.append(wide_grad[size : 2 * size] * scale)
        bins = wide_grad[2 * size : 2 * size + LEVELS]
        top = bins.astype(half)
        rest = (bins - top.astype(single)).astype(half)
        sums = times(top, keyx) + times(rest, keyx)
        part = slice(which * LEVELS, (which + 1) * LEVELS)
        sums_ref[0, part, :] = sums if first else sums + old_sums_ref[0, part, :]
    rows_ref[0] = jnp.transpose(jnp.concatenate(gq, axis=0)).astype(half)
    rows_ref[1] = jnp.concatenate(gk, axis=1).astype(half)
    rows_ref[2] = jnp.concatenate(gv, axis=1).astype(half)
    cell_q = times(cells_t, jnp.transpose(jnp.concatenate(gsq, axis=0)).astype(half))
    cell_k = times(cells_t, jnp.concatenate(gsk, axis=1).astype(half))
    cell_q_ref[...] = cell_q if first else cell_q + old_q_ref[...]
    cell_k_ref[...] = cell_k if first else cell_k + old_k_ref[...]


def attend_page_back(
    page, joint_half, spatial_rows, cells, cells_t, keyx, rel, log_total, grad, out_w, heads, before
):
    tokens = joint_half.shape[0]
    width = out_w.shape[0]
    size = width // heads
    pairs = heads // PAIR
    block = PAIR * size
    table_rows = spatial_rows.shape[0]
    cells_out = pl.BlockSpec((table_rows, block), lambda h: (0, h))
    sums_out = pl.BlockSpec((1, PAIR * LEVELS, LANES), lambda h: (h, 0, 0))
    first = before is None
    more = [] if first else [pl.BlockSpec(memory_space=pltpu.HBM), cells_out, cells_out, sums_out]
    return pl.pallas_call(
        functools.partial(backward_kernel, scale=size**-0.5, size=size, first=first),
        grid=(pairs,),
        in_specs=[
            pl.BlockSpec((SLOTS, block), lambda h: (page, h)),
            pl.BlockSpec((SLOTS, block), lambda h: (page, pairs + h)),
            pl.BlockSpec((SLOTS, block), lambda h: (page, 2 * pairs + h)),
            pl.BlockSpec((table_rows, block), lambda h: (0, h)),
            pl.BlockSpec((table_rows, block), lambda h: (0, pairs + h)),
            pl.BlockSpec((SLOTS, table_rows), lambda h: (page, 0)),
            pl.BlockSpec((table_rows, SLOTS), lambda h: (0, page)),
            pl.BlockSpec((SLOTS, LANES), lambda h: (page, 0)),
            pl.BlockSpec((LANES, PAIR * LANES), lambda h: (0, h)),
            pl.BlockSpec((heads, SLOTS), lambda h: (0, 0)),
            pl.BlockSpec((SLOTS, width), lambda h: (0, 0)),
            pl.BlockSpec((block, width), lambda h: (h, 0)),
            *more,
        ],
        out_specs=[
            pl.BlockSpec((3, SLOTS, block), lambda h: (0, page, h)), cells_out, cells_out, sums_out
        ],
        out_shape=[
            jax.ShapeDtypeStruct((3, tokens, width), half),
            jax.ShapeDtypeStruct((table_rows, width), single),
            jax.ShapeDtypeStruct((table_rows, width), single),
            jax.ShapeDtypeStruct((pairs, PAIR * LEVELS, LANES), single),
        ],
        input_output_aliases={} if first else {12: 0, 13: 1, 14: 2, 15: 3},
        compiler_params=pltpu.CompilerParams(vmem_limit_bytes=32 << 20),
        cost_estimate=pl.CostEstimate(
            flops=2 * heads * SLOTS * SLOTS * 16 * size,
            bytes_accessed=20 * SLOTS * width,
            transcendentals=heads * SLOTS * SLOTS,
        ),
        name="attend_page_back",
    )(
        joint_half, joint_half, joint_half, spatial_rows, spatial_rows, cells, cells_t, keyx, rel,
        log_total, grad, out_w, *(before or ()),
    )


def input_grad_kernel(rows_ref, weight_ref, resid_ref, out_ref):
    part = times_transposed(rows_ref[0], weight_ref[...])

    @pl.when(pl.program_id(0) == 0)
    def _():
        out_ref[...] = resid_ref[...] + part

    @pl.when(pl.program_id(0) > 0)
    def _():
        out_ref[...] += part


def input_grad(rows, weight, resid):
    parts, tokens, width = rows.shape
    return pl.pallas_call(
        input_grad_kernel,
        grid=(parts,),
        in_specs=[
            pl.BlockSpec((1, tokens, width), lambda n: (n, 0, 0)),
            pl.BlockSpec((width, width), lambda n: (0, n)),
            pl.BlockSpec((tokens, width), lambda n: (0, 0)),
        ],
        out_specs=pl.BlockSpec((tokens, width), lambda n: (0, 0)),
        out_shape=jax.ShapeDtypeStruct((tokens, width), single),
        compiler_params=pltpu.CompilerParams(vmem_limit_bytes=32 << 20),
        cost_estimate=pl.CostEstimate(
            flops=2 * parts * tokens * width * width,
            bytes_accessed=14 * tokens * width,
            transcendentals=0,
        ),
        name="input_grad",
    )(rows, weight, resid)


def level_offsets():
    row_bin = lax.broadcasted_iota(jnp.int32, (BINS, BINS, SPAN), 0)
    col_bin = lax.broadcasted_iota(jnp.int32, (BINS, BINS, SPAN), 1)
    offset = lax.broadcasted_iota(jnp.int32, (BINS, BINS, SPAN), 2)
    return (col_bin - row_bin + BINS - 1 == offset).astype(single)


def relative_columns(relative, offsets):
    heads = relative.shape[0]
    tables = relative.reshape(heads, 3, SPAN)
    squares = jnp.einsum("hfr,acr->fahc", tables, offsets, precision=highest)
    blocks = jnp.zeros((3, BINS, heads, 3, BINS), single)
    for family in range(3):
        blocks = blocks.at[family, :, :, family].set(squares[family])
    blocks = blocks.reshape(LEVELS, heads, LEVELS)
    top = blocks.astype(half)
    low = (blocks - top.astype(single)).astype(half)
    ones = (lax.broadcasted_iota(jnp.int32, (LEVELS, heads, 1), 0) < BINS).astype(half)
    spare = jnp.zeros((LEVELS, heads, LANES - 2 * LEVELS - 1), half)
    columns = jnp.concatenate([top, low, ones, spare], -1).reshape(LEVELS, heads * LANES)
    return jnp.pad(columns, ((0, LANES - LEVELS), (0, 0)))


def key_columns(bins, key_valid):
    tokens = bins.shape[1]
    level = lax.broadcasted_iota(jnp.int32, (tokens, BINS), 1)
    onehot = jnp.concatenate([(bins[f][:, None] == level).astype(half) for f in range(3)], -1)
    masked = jnp.where(key_valid > 0, 0.0, masked_score).astype(half)[:, None]
    spare = jnp.zeros((tokens, LANES - 2 * LEVELS - 1), half)
    return jnp.concatenate([onehot, onehot, masked, spare], -1)


def relative_grad(sums, offsets):
    pairs = sums.shape[0]
    sums = sums.reshape(pairs * PAIR, LEVELS, LANES)[:, :, :LEVELS]
    pieces = []
    for family in range(3):
        part = slice(family * BINS, (family + 1) * BINS)
        pieces.append(jnp.einsum("hca,acr->hr", sums[:, part, part], offsets, precision=highest))
    return jnp.concatenate(pieces, -1)


def body(
    features,
    box_bins,
    text_mask,
    spatial_table,
    joint_projection,
    spatial_projection,
    relative_table,
    output_projection,
    output_bias,
    norm_one_gain,
    norm_one_shift,
    up_weight,
    up_bias,
    down_weight,
    down_bias,
    norm_two_gain,
    norm_two_shift,
    output_cotangent,
    *,
    count,
):
    tokens, width = features.shape[1:]
    heads = relative_table.shape[1]
    table_rows = spatial_table.shape[0]
    page_count = tokens // SLOTS
    stream_side = lax.axis_index("stream")
    key_valid = jnp.where(stream_side == 0, text_mask, jnp.ones_like(text_mask))
    inputs = features[0]
    bins = box_bins[0]
    gain_one, shift_one = norm_one_gain[0], norm_one_shift[0]
    gain_two, shift_two = norm_two_gain[0], norm_two_shift[0]

    early = jnp.concatenate([joint_projection, spatial_projection, output_projection], -1)
    early = lax.all_gather(early, "pages", axis=1, tiled=True)[0]
    full_joint = early[:, : 3 * width]
    full_spatial = early[:, 3 * width : 5 * width]
    full_output = early[:, 5 * width :]
    full_up = lax.all_gather(up_weight, "pages", axis=1, tiled=True)[0]
    full_down = lax.all_gather(down_weight, "pages", axis=1, tiled=True)[0]

    offsets = level_offsets()
    rel = relative_columns(relative_table[0], offsets)
    keyx = key_columns(bins, key_valid)
    cell_ids = bins[2] * BINS + bins[1]
    cells = (cell_ids[:, None] == lax.broadcasted_iota(jnp.int32, (tokens, table_rows), 1)).astype(half)
    cells_t = (cell_ids[None, :] == lax.broadcasted_iota(jnp.int32, (table_rows, tokens), 0)).astype(half)

    joint_half = times(inputs, full_joint).astype(half)
    spatial_rows = times(spatial_table, full_spatial).astype(half)
    mixtures, logs, joined = [], [], []
    for page in range(page_count):
        mixture, own, sent, log_total = attend_page(
            page, joint_half, spatial_rows, cells, keyx, rel, full_output, output_bias, heads
        )
        mixtures.append(mixture)
        logs.append(log_total)
        joined.append(own + swap_streams(sent).astype(single))
    mixture = jnp.concatenate(mixtures, 0)
    joined = jnp.concatenate(joined, 0)

    normed_one, inverse_one = layer_stats(inputs.astype(single) + joined)
    hidden = normed_one * gain_one + shift_one
    hidden_half = hidden.astype(half)
    activated, slope = gelu_slope(times(hidden_half, full_up) + up_bias[0])
    active_half = activated.astype(half)
    normed_two, inverse_two = layer_stats(hidden + (times(active_half, full_down) + down_bias[0]))
    layer_output = (normed_two * gain_two + shift_two).astype(half)
    upstream = output_cotangent[0].astype(single)
    grad_resid_two = norm_back(upstream * gain_two, normed_two, inverse_two)
    grad_branch = grad_resid_two.astype(half)
    down_sum = RowSum(active_half, grad_branch, count, width, by_rows=True)
    grad_branch = after(grad_branch, down_sum)
    down_sum.cores()
    grad_pre = (times_transposed(grad_branch, full_down) * slope).astype(half)
    grad_pre = after(grad_pre, down_sum)
    down_sum.across_x()
    grad_hidden = grad_resid_two + times_transposed(grad_pre, full_up)
    grad_resid_one = norm_back(grad_hidden * gain_one, normed_one, inverse_one)
    sent, hidden_back = lax.optimization_barrier((grad_resid_one.astype(half), hidden_half))
    up_sum = RowSum(hidden_back, grad_pre, count, width)

    grad_attention, before = [], None
    for page in range(page_count):
        rows = slice(page * SLOTS, (page + 1) * SLOTS)
        part = grad_resid_one[rows] + swap_streams(sent[rows]).astype(single)
        grad_attention.append(part.astype(half))
    up_sum.cores()
    grad_attention[0] = after(grad_attention[0], down_sum, up_sum)
    down_sum.across_z()
    up_sum.across_x()
    output_sum = None
    for page in range(page_count):
        part = grad_attention[page]
        if page == page_count - 1:
            output_sum = RowSum(mixture, jnp.concatenate(grad_attention, 0), count, width)
            part = after(part, down_sum, output_sum)
            output_sum.cores()
        before = attend_page_back(
            page, joint_half, spatial_rows, cells, cells_t, keyx, rel, logs[page], part, full_output,
            heads, before,
        )
    grad_rows, cell_q, cell_k, bin_sums = before
    grad_attention = jnp.concatenate(grad_attention, 0)
    grad_rows = after(grad_rows, up_sum, output_sum)
    up_sum.across_z()
    joint_sum = RowSum(inputs, grad_rows, count, width)
    cell_half = jnp.concatenate([cell_q, cell_k], 1).astype(half)
    cell_half = after(cell_half, joint_sum)
    joint_sum.cores()
    spatial_sum = RowSum(spatial_table, cell_half, count, width)
    cell_half = after(cell_half, joint_sum, spatial_sum)
    joint_sum.across_x()
    spatial_sum.cores()
    output_sum.across_x()
    spatial_sum.across_x()
    joint_sum.across_z()
    output_sum.across_z()
    spatial_sum.across_z()
    grad_table = sum_table(times_transposed(cell_half, full_spatial), count)
    grad_rows = lax.optimization_barrier((grad_rows, cell_half))[0]
    grad_features = input_grad(grad_rows, full_joint, grad_resid_one)

    small = [
        jnp.sum(grad_hidden * normed_one, 0),
        jnp.sum(grad_hidden, 0),
        jnp.sum(grad_attention.astype(single), 0),
        jnp.sum(grad_pre.astype(single), 0),
        jnp.sum(grad_branch.astype(single), 0),
        jnp.sum(upstream * normed_two, 0),
        jnp.sum(upstream, 0),
        relative_grad(bin_sums, offsets).reshape(-1),
    ]
    ends = []
    for piece in small:
        ends.append((ends[-1] if ends else 0) + piece.shape[0])
    packed = jnp.concatenate(small)
    packed = jnp.pad(packed, (0, -ends[-1] % (8 * LANES))).reshape(-1, LANES)
    packed = sum_pages(packed, count, single).reshape(-1)
    small = [packed[end - piece.shape[0] : end] for end, piece in zip(ends, small)]

    return (
        layer_output[None],
        grad_features[None],
        joint_sum.result(),
        spatial_sum.result(),
        small[7].reshape(relative_table.shape),
        output_sum.result(),
        small[2][None],
        small[0][None],
        small[1][None],
        up_sum.result(),
        small[3][None],
        down_sum.result(),
        small[4][None],
        small[5][None],
        small[6][None],
        grad_table,
    )


def solution(mesh):
    rows = P("stream", "pages", None)
    vector = P("stream", None)
    placed = (
        rows,
        P("stream", None, "pages"),
        P("pages"),
        P(),
        rows,
        rows,
        P("stream", None, None),
        rows,
        vector,
        vector,
        vector,
        rows,
        vector,
        rows,
        vector,
        vector,
        vector,
        rows,
    )
    out_specs = (
        rows,
        rows,
        rows,
        rows,
        P("stream", None, None),
        rows,
        vector,
        vector,
        vector,
        rows,
        vector,
        rows,
        vector,
        vector,
        vector,
        P(),
    )
    return jax.shard_map(
        functools.partial(body, count=mesh.shape["pages"]),
        mesh=mesh,
        in_specs=placed,
        out_specs=out_specs,
        check_vma=False,
    )
```
